32 devices in a mesh: grp: 4 (over z), mem: 8 (over y, x, core).
Axes of the slice: x: 2, y: 2, z: 4, core: 2. Of those that a mesh axis runs over, the one named last changes fastest.
Arguments:
- bin_sketch: bfloat16 [256, 1024], P(('grp', 'mem')), may hold values from -6 to 6
- rep_sketch: bfloat16 [8192, 1024], P(('grp', 'mem')), may hold values from -6 to 6
- bin_profile: bfloat16 [256, 32768], P('grp', 'mem'), may hold values from -6 to 6
- member_profile: bfloat16 [12, 256, 32768], P('grp', None, 'mem'), may hold values from -6 to 6
- bin_routes: int32 [256, 2], P('grp'), may hold values from 0 to 11, all different within a row; in each aligned block of 64 rows (0 to 63, 64 to 127, ...) at most 16 rows name the same one
- owner_slot: int32 [12], replicated, may hold values from 0 to 11, each once
- cluster_sizes: int32 [12], replicated, may hold values from 128 to 256, as said below
Outputs:
- coarse_scores: bfloat16 [256, 8192], P(None, ('grp', 'mem'))
- fine_scores: float32 [256, 2, 256], P('grp', None, 'mem')
The draws below stay inside these ranges and needn't reach their ends.
Inputs may be any that keep to these rules, and one draw needn't show every extreme that they name: `bin_routes`: within the bins of one index of grp (64 consecutive bins), no cluster is named by more than 16 routes, a bound that some block reaches; the two clusters of a bin differ. `owner_slot`: A permutation. `cluster_sizes`: each a multiple of 128.
All inputs are finite; a program needn't handle non-finite values.
Results may differ from the reference program's by a relative error of at most 0.001.
Values may be sent and summed in bfloat16 or wider, within the bound.
No kernel may reach another device: no remote copies, remote signals or barrier semaphores. Data moves between devices by JAX's collectives and lax.ppermute only.
A program may use at most 128 MiB of HBM per device.

```python
import math
import jax
import jax.numpy as jnp
import numpy as np
from jax import lax

W = 1024
FW = 32768
MEMBERS = 256
BIN_DEV = 8
BINS = 256
REPS = 8192
CLUSTERS = 12
MOST = 16
BLOCK = 128
N_GRP = 4
N_MEM = 8


def draw_cluster_sizes(key, part):
    first_key = jax.random.fold_in(key, 11)
    second_key = jax.random.fold_in(key, 12)
    third_key = jax.random.fold_in(key, 13)
    blocks_each = jax.random.randint(first_key, (CLUSTERS,), 1, 3)
    small_one = jax.random.randint(second_key, (), 0, CLUSTERS)
    large_one = (small_one + 1 + jax.random.randint(third_key, (), 0, CLUSTERS - 1)) % CLUSTERS
    position = jnp.arange(CLUSTERS)
    blocks_each = jnp.where(position == small_one, 1, blocks_each)
    blocks_each = jnp.where(position == large_one, 2, blocks_each)
    return (blocks_each * BLOCK).astype(jnp.int32)


def block_scale(own_key, dims, split, low, largest):
    def one(axis_at, blocks):
        steps = jax.random.uniform(jax.random.fold_in(jax.random.fold_in(own_key, 6), axis_at), (blocks,), jnp.float32, low / len(split), largest / len(split))
        return jnp.repeat(jnp.exp(steps), dims[axis_at] // blocks).reshape((-1,) + (1,) * (len(dims) - axis_at - 1))

    gain = one(*split[0])
    for cut in split[1:]:
        gain = gain * one(*cut)
    return gain


def routed_block(key, own, number, rows, count, top, most, skew):
    order = jax.random.permutation(key, count)
    packed, usual = portions_of(count, rows * top, most, skew, True), portions_of(count, rows * top, most, skew, False)
    places = jnp.arange(count)

    def named(lengths, rotation):
        used = int((lengths > 0).sum())
        fixed = max(1, used // 4)
        moved = fixed + (places - fixed + rotation * (used - fixed)) % max(1, count - fixed)
        return jnp.zeros((count,), jnp.int32).at[order[jnp.where(places < fixed, places, moved)]].set(jnp.asarray(lengths, jnp.int32))

    lengths = jnp.where(number % 4 == 0, named(packed, number // 4), named(usual, number - number // 4 - 1))
    mixed = jax.random.permutation(jax.random.fold_in(own, 3), count)
    giver, sink = mixed[0:count // 2 * 2:2], mixed[1:count // 2 * 2:2]
    slack = jnp.minimum(lengths[giver] - 1, most - lengths[sink]) // 2
    slack = jnp.where((giver == order[0]) | (sink == order[0]) | (lengths[sink] == 0), 0, jnp.maximum(slack, 0))
    moved = jax.random.randint(jax.random.fold_in(own, 4), (count // 2,), 0, 1 << 20) % (slack + 1)
    lengths = lengths.at[giver].add(-moved).at[sink].add(moved)
    members = jnp.searchsorted(jnp.cumsum(lengths), jnp.arange(rows * top), side="right").astype(jnp.int32)
    listing = members.reshape(top, rows).T
    listing = listing[jax.random.permutation(jax.random.fold_in(own, 1), rows)]
    rotation = jax.random.randint(jax.random.fold_in(own, 2), (rows, 1), 0, top)
    return jnp.take_along_axis(listing, (jnp.arange(top)[None, :] + rotation) % top, axis=1)


def portions_of(number_of, total, limit, slope, full):
    loads = [(1 << 20) // math.isqrt(grade ** slope) + 1 for grade in range(1, number_of + 1)]
    largest = limit if full else min(limit, max(-(-total // number_of), total * loads[0] // sum(loads)))
    least = 1 if total - largest >= number_of - 1 else 0
    given, surplus = [largest] + [least] * (number_of - 1), total - largest - least * (number_of - 1)
    while surplus > 0:
        free = [i for i in range(1, number_of) if given[i] < largest] or [i for i in range(1, number_of) if given[i] < limit]
        whole, budget = sum([loads[i] for i in free]), surplus
        for i in free:
            more = min(limit - given[i], max(1, budget * loads[i] // whole), surplus)
            given[i] = given[i] + more
            surplus = surplus - more
    return np.array(given)


def scatter_about(rng, dims, scale, bound, split=(), kind=jnp.bfloat16):
    entries = scale * jax.random.normal(rng, dims, jnp.float32)
    if split:
        entries = entries * block_scale(rng, dims, split, -0.22, 0.18)
    return jnp.clip(entries, -bound, bound).astype(kind)


def setup_inputs(seed: int = 0) -> dict:
    arg_keys = jax.random.split(jax.random.key(seed), 8)
    bin_sketch = scatter_about(arg_keys[0], (BINS, W), 1.0, 6.0, ((0, 32),))
    rep_sketch = scatter_about(arg_keys[1], (REPS, W), 1.0, 6.0, ((0, 32),))
    bin_profile = scatter_about(arg_keys[2], (BINS, FW), 1.0, 6.0, ((0, 4), (1, 8)))
    member_profile = scatter_about(arg_keys[3], (CLUSTERS, MEMBERS, FW), 1.0, 6.0, ((0, 4), (2, 8)))
    bin_routes_keys = jax.random.split(jax.random.fold_in(arg_keys[4], 1), BINS // (BIN_DEV * N_MEM))
    bin_routes_turns = jax.random.permutation(jax.random.fold_in(arg_keys[4], 3), BINS // (BIN_DEV * N_MEM))
    bin_routes = jax.vmap(lambda own, number: routed_block(jax.random.fold_in(arg_keys[4], 2), own, number, BIN_DEV * N_MEM, CLUSTERS, 2, MOST, 2))(bin_routes_keys, bin_routes_turns).reshape((BINS, 2))
    owner_slot = jax.random.permutation(arg_keys[5], CLUSTERS).astype(jnp.int32)
    cluster_sizes = draw_cluster_sizes(jax.random.fold_in(arg_keys[7], 71), 0)
    return {"bin_sketch": bin_sketch, "rep_sketch": rep_sketch, "bin_profile": bin_profile, "member_profile": member_profile, "bin_routes": bin_routes, "owner_slot": owner_slot, "cluster_sizes": cluster_sizes}


def reference(bin_sketch, rep_sketch, bin_profile, member_profile, bin_routes, owner_slot, cluster_sizes):
    coarse_scale = W ** -0.5

    def coarse_block(rows_block):
        product = lax.dot_general(rows_block, rep_sketch, (((1,), (1,)), ((), ())), preferred_element_type=jnp.float32)
        return (product * coarse_scale).astype(jnp.bfloat16)

    block_count = max(BINS // 256, 1)
    blocks = bin_sketch.reshape(block_count, BINS // block_count, W)
    coarse_scores = lax.map(coarse_block, blocks).reshape(BINS, REPS)

    route_flat = bin_routes.reshape(-1)
    route_slot = owner_slot[route_flat]
    capacity = N_GRP * MOST

    def per_cluster(slot_now):
        route_hit = route_slot == slot_now
        picked = jnp.argsort(jnp.where(route_hit, 0, 1).astype(jnp.int32), stable=True)[:capacity].astype(jnp.int32)
        profiles = bin_profile[picked // 2]
        product = lax.dot_general(profiles, member_profile[slot_now], (((1,), (1,)), ((), ())), preferred_element_type=jnp.float32)
        return picked, jnp.where(route_hit[picked][:, None], product, 0.0)

    picked_all, product_all = lax.map(per_cluster, jnp.arange(CLUSTERS, dtype=jnp.int32))
    raw_scores = jnp.zeros((2 * BINS, MEMBERS), jnp.float32).at[picked_all.reshape(-1)].add(product_all.reshape(-1, MEMBERS))
    member_index = jnp.arange(MEMBERS, dtype=jnp.int32)
    member_live = member_index[None, :] < cluster_sizes[route_flat][:, None]
    fine_scores = jnp.where(member_live, raw_scores * (FW ** -0.5), 0.0).reshape(BINS, 2, MEMBERS)
    return coarse_scores, fine_scores
```

```python
import jax
import jax.numpy as jnp
from jax import lax
from jax.sharding import PartitionSpec as P

FW = 32768
MOST = 16


def pick(hit, rows):
    return lax.dot_general(
        hit.astype(jnp.bfloat16),
        rows,
        (((1,), (0,)), ((), ())),
        preferred_element_type=jnp.float32,
    ).astype(jnp.bfloat16)


def make_local(groups, mems):
    last = groups - 1
    half = groups // 2
    middle = (half - 1, half) if groups > 1 else ()

    def swap(value, key):
        return lax.ppermute(value, "grp", [(i, i ^ key) for i in range(groups)])

    def local(
        bin_sketch, rep_sketch, bin_profile, member_profile, bin_routes, owner_slot, cluster_sizes
    ):
        rows_here, width_here = bin_profile.shape
        slot_count, members, _ = member_profile.shape
        per_group = slot_count * MOST
        me = lax.axis_index("grp")
        mine = lax.axis_index("mem")
        inner = (me == half - 1) | (me == half)

        whole = lax.ppermute(
            bin_profile, "grp", [(i, i ^ last) for i in range(groups) if i in middle]
        )

        cluster_ids = jnp.arange(owner_slot.shape[0], dtype=jnp.int32)
        route_flat = bin_routes.T.reshape(-1)
        route_hit = (route_flat[None, :] == cluster_ids[:, None]).astype(jnp.int32)
        storage = jnp.sum(route_hit * owner_slot[:, None], axis=0)
        route_size = jnp.sum(route_hit * cluster_sizes[:, None], axis=0)
        route_rank = jnp.sum((jnp.cumsum(route_hit, axis=1) - route_hit) * route_hit, axis=0)
        place = (storage * MOST + route_rank).reshape(2, rows_here)
        place_other = swap(place, last)

        local_place = jnp.arange(per_group, dtype=jnp.int32)[:, None]

        def chosen(where, group, rows):
            wanted = local_place + group * per_group
            return pick((where[0][None] == wanted) | (where[1][None] == wanted), rows)

        def scores(rows):
            split = rows.reshape(slot_count, MOST, width_here)
            out = lax.dot_general(
                member_profile,
                split,
                (((2,), (2,)), ((0,), (0,))),
                preferred_element_type=jnp.float32,
            )
            return out.transpose(1, 0, 2).reshape(members, per_group)

        def reduce_mem(value):
            step = 1
            block = members // mems
            value = value.reshape(mems, block, value.shape[1])
            while step < mems:
                bit = (mine // step) % 2
                pairs = value.reshape(value.shape[0] // 2, 2, block, value.shape[2])
                keep = lax.dynamic_index_in_dim(pairs, bit, 1, keepdims=False)
                send = lax.dynamic_index_in_dim(pairs, 1 - bit, 1, keepdims=False)
                got = lax.ppermute(send, "mem", [(i, i ^ step) for i in range(mems)])
                value = keep + got
                step *= 2
            return value.reshape(block, -1)

        sent = {}
        for key in range(1, half):
            sent[key] = swap(chosen(place, me ^ key, bin_profile), key)
        if groups > 1:
            outer = [(i, i ^ last) for i in range(groups) if i not in middle]
            direct = lax.ppermute(chosen(place, me ^ last, bin_profile), "grp", outer)
            sent[last] = jnp.where(inner, chosen(place_other, me, whole), direct)
        for key in range(half, last):
            there = jnp.where(inner, me ^ last ^ key, me ^ key)
            block = jnp.where(inner, whole, bin_profile)
            where = jnp.where(inner, place_other, place)
            route = [(i, i ^ last ^ key if i in middle else i ^ key) for i in range(groups)]
            sent[key] = lax.ppermute(chosen(where, there, block), "grp", route)
        sent[0] = chosen(place, me, bin_profile)

        sketches = lax.all_gather(bin_sketch, "grp", axis=0)
        sketches = lax.all_gather(sketches, "mem", axis=0)
        product = lax.dot_general(
            sketches.transpose(1, 0, 2, 3).reshape(-1, sketches.shape[3]),
            rep_sketch,
            (((1,), (1,)), ((), ())),
            preferred_element_type=jnp.float32,
        )
        coarse_scores = (product * bin_sketch.shape[1] ** (-0.5)).astype(jnp.bfloat16)

        early = [k for k in range(groups) if k < half]
        late = [k for k in range(groups) if k >= half]
        back = {}
        for keys in (early, late):
            if keys:
                summed = reduce_mem(jnp.concatenate([scores(sent[k]) for k in keys], axis=1))
                for at, k in enumerate(keys):
                    part = summed[:, at * per_group : (at + 1) * per_group]
                    back[k] = swap(part, k) if k else part
        table = jnp.concatenate([back[k] for k in range(groups)], axis=1)

        owner = place // per_group
        column = (owner ^ me) * per_group + place % per_group
        ids = jnp.arange(groups * per_group, dtype=jnp.int32)[:, None]
        found = (column.reshape(-1)[None, :] == ids).astype(jnp.float32)
        raw = lax.dot_general(
            table,
            found,
            (((1,), (0,)), ((), ())),
            precision=lax.Precision.HIGHEST,
            preferred_element_type=jnp.float32,
        )
        member_local = table.shape[0]
        member = mine * member_local + jnp.arange(member_local, dtype=jnp.int32)
        live = member[:, None] < route_size[None, :]
        fine = jnp.where(live, raw * FW ** (-0.5), 0.0)
        fine_scores = fine.reshape(member_local, 2, rows_here).transpose(2, 1, 0)
        return (coarse_scores, fine_scores)

    return local


def solution(mesh):
    return jax.shard_map(
        make_local(mesh.shape["grp"], mesh.shape["mem"]),
        mesh=mesh,
        in_specs=(
            P(("grp", "mem"), None),
            P(("grp", "mem"), None),
            P("grp", "mem"),
            P("grp", None, "mem"),
            P("grp", None),
            P(),
            P(),
        ),
        out_specs=(P(None, ("grp", "mem")), P("grp", None, "mem")),
        check_vma=False,
    )
```

```python
import functools

import jax
import jax.numpy as jnp
from jax import lax
from jax.experimental import pallas as pl
from jax.experimental.pallas import tpu as pltpu
from jax.sharding import PartitionSpec as P

FW = 32768
MOST = 16
VM = pl.BlockSpec(memory_space=pltpu.VMEM)
SM = pl.BlockSpec(memory_space=pltpu.SMEM)
NT = (((1,), (1,)), ((), ()))
NN = (((1,), (0,)), ((), ()))


def iota(shape, axis):
    return lax.broadcasted_iota(jnp.int32, shape, axis)


def hits(where, group, count):
    wanted = iota((count, where.shape[1]), 0) + group * count
    return (where[0:1] == wanted) | (where[1:2] == wanted)


def pick(hit, rows):
    one = hit.astype(jnp.float32).astype(jnp.bfloat16)
    return lax.dot_general(one, rows, NN, preferred_element_type=jnp.float32).astype(jnp.bfloat16)


def index_kernel(count, who, slots, sizes, routes, places, lives):
    total = slots.shape[0]
    rows = routes.shape[1]
    cluster = iota((total, rows), 0)
    slot_of = jnp.zeros((total, rows), jnp.int32)
    size_of = jnp.zeros((total, rows), jnp.int32)
    for c in range(total):
        slot_of = jnp.where(cluster == c, slots[c], slot_of)
        size_of = jnp.where(cluster == c, sizes[c], size_of)
    before = (iota((rows, rows), 0) < iota((rows, rows), 1)).astype(jnp.float32).astype(jnp.bfloat16)
    seen = jnp.zeros((total, 1), jnp.float32)
    for r in range(2):
        hit = routes[r : r + 1] == cluster
        one = hit.astype(jnp.float32)
        earlier = lax.dot_general(
            one.astype(jnp.bfloat16), before, NN, preferred_element_type=jnp.float32
        )
        rank = jnp.sum(jnp.where(hit, earlier + seen, 0.0), axis=0, keepdims=True)
        seen = seen + jnp.sum(one, axis=1, keepdims=True)
        slot = jnp.sum(jnp.where(hit, slot_of, 0), axis=0, keepdims=True)
        places[r : r + 1] = slot * MOST + rank.astype(jnp.int32)
        lives[r : r + 1] = jnp.sum(jnp.where(hit, size_of, 0), axis=0, keepdims=True)


def pick_kernel(count, groups, who, places, rows, *outs):
    where = places[...]
    for group, out in zip(groups, outs, strict=True):
        out[...] = pick(hits(where, who[group], count), rows[...])


def forward_kernel(count, keys, who, places, places_other, rows, whole, *outs):
    @pl.when(who[0] == 1)
    def _():
        where = places_other[...]
        for at in range(keys):
            outs[at][...] = pick(hits(where, who[1 + at], count), whole[...])
        outs[keys][...] = pick(hits(where, who[1 + keys], count), whole[...])

    @pl.when(who[0] == 0)
    def _():
        where = places[...]
        for at in range(keys):
            outs[at][...] = pick(hits(where, who[1 + at], count), rows[...])


def score_kernel(n_in, choose, mems, who, members, *refs):
    ins, (keep, send, acc) = refs[:n_in], refs[n_in:]
    slot_count, total, _ = members.shape
    count = slot_count * MOST
    block = total // mems

    def put(src, lane):
        for s in range(slot_count):
            acc[:, lane + s * MOST : lane + (s + 1) * MOST] = lax.dot_general(
                members[s], src[s * MOST : (s + 1) * MOST, :], NT, preferred_element_type=jnp.float32
            )

    lane = 0
    for at in range(n_in - (1 if choose else 0)):
        if choose and at == n_in - 2:
            @pl.when(who[0] == 1)
            def _(lane=lane, at=at):
                put(ins[at], lane)

            @pl.when(who[0] == 0)
            def _(lane=lane, at=at):
                put(ins[at + 1], lane)
        else:
            put(ins[at], lane)
        lane += count
    for p in range(mems // 2):
        for core, out in ((0, keep), (1, send)):
            at = (who[1] ^ (p * 2 + core)) * block
            out[p] = acc[pl.ds(pl.multiple_of(at, block), block), :]


def final_kernel(count, scale, keys, who, places, lives, *refs):
    tables, out = refs[:-1], refs[-1]
    block, rows = out.shape[1], out.shape[2]
    member = iota((block, rows), 0) + who[0]
    for r in range(2):
        total = jnp.zeros((block, rows), jnp.float32)
        where = places[r : r + 1]
        for at in range(len(keys)):
            wanted = iota((count, rows), 0) + who[1 + at] * count
            one = (where == wanted).astype(jnp.float32)
            total = total + lax.dot_general(
                tables[at][...], one, NN,
                precision=lax.Precision.HIGHEST, preferred_element_type=jnp.float32,
            )
        out[r] = jnp.where(member < lives[r : r + 1], total * scale, 0.0)


def call(kernel, shapes, n_smem, n_vmem, scratch=(), name=None, flops=0):
    return pl.pallas_call(
        kernel,
        out_shape=[jax.ShapeDtypeStruct(s, d) for s, d in shapes],
        in_specs=[SM] * n_smem + [VM] * n_vmem,
        out_specs=[VM] * len(shapes),
        scratch_shapes=scratch,
        name=name,
        cost_estimate=pl.CostEstimate(flops=flops, bytes_accessed=1 << 18, transcendentals=0),
    )


def make_local(groups, mems):
    last = groups - 1
    half = groups // 2
    middle = (half - 1, half)

    def swap(value, key):
        return lax.ppermute(value, "grp", [(i, i ^ key) for i in range(groups)])

    def swap_mem(value, key):
        return lax.ppermute(value, "mem", [(i, i ^ key) for i in range(mems)])

    def local(
        bin_sketch, rep_sketch, bin_profile, member_profile, bin_routes, owner_slot, cluster_sizes
    ):
        rows_here, width_here = bin_profile.shape
        slot_count, members, _ = member_profile.shape
        count = slot_count * MOST
        block = members // mems
        me = lax.axis_index("grp")
        mine = lax.axis_index("mem")
        inner = ((me == half - 1) | (me == half)).astype(jnp.int32)
        bf, f32, i32 = jnp.bfloat16, jnp.float32, jnp.int32
        rows_out = ((count, width_here), bf)

        with jax.named_scope("whole"):
            whole = lax.ppermute(bin_profile, "grp", [(i, i ^ last) for i in middle])

        near = list(range(1, half))
        far = list(range(half, last))
        with jax.named_scope("index"):
            places, lives = call(
                functools.partial(index_kernel, count),
                [((2, rows_here), i32)] * 2, 3, 1, name="index",
            )(me.reshape(1), owner_slot, cluster_sizes, bin_routes.T)
        with jax.named_scope("place"):
            places_other = swap(places, last)
        with jax.named_scope("picks"):
            who = jnp.stack([me ^ k for k in near + [last, 0]])
            *sends, own = call(
                functools.partial(pick_kernel, count, range(len(near) + 2)),
                [rows_out] * (len(near) + 2), 1, 2, name="picks",
            )(who, places, bin_profile)

        sketches = bin_sketch[None]
        with jax.named_scope("sketch_grp"):
            sketches = jnp.stack([bin_sketch] + [swap(bin_sketch, k) for k in range(1, groups)])

        got = {0: own}
        with jax.named_scope("near"):
            for k in near:
                got[k] = swap(sends[k - 1], k)
        with jax.named_scope("direct"):
            outer = [(i, i ^ last) for i in range(groups) if i not in middle]
            direct = lax.ppermute(sends[-1], "grp", outer) if outer else sends[-1]
        with jax.named_scope("forward"):
            who = jnp.stack([inner] + [jnp.where(inner == 1, me ^ last ^ k, me ^ k) for k in far] + [me])
            *onward, through = call(
                functools.partial(forward_kernel, count, len(far)),
                [rows_out] * (len(far) + 1), 1, 4, name="forward",
            )(who, places, places_other, bin_profile, whole)
        with jax.named_scope("far"):
            for at, k in enumerate(far):
                way = [(i, i ^ last ^ k if i in middle else i ^ k) for i in range(groups)]
                got[k] = lax.ppermute(onward[at], "grp", way)

        step = 1
        while step < mems:
            with jax.named_scope("sketch_mem"):
                sketches = jnp.stack([sketches, swap_mem(sketches, step)])
            step *= 2
        sketches = sketches.reshape(-1, bin_sketch.shape[1])

        def scores(arrays, choose):
            lanes = count * (len(arrays) - choose)
            return call(
                functools.partial(score_kernel, len(arrays), choose, mems),
                [((mems // 2, block, lanes), f32)] * 2, 1, 1 + len(arrays),
                scratch=[pltpu.VMEM((members, lanes), f32)], name="scores",
                flops=2 * members * width_here * lanes * 8,
            )(jnp.stack([inner, mine]), member_profile, *arrays)

        def reduce_mem(keep, send):
            value = keep + swap_mem(send, 1)
            while value.shape[0] > 1:
                n = value.shape[0] // 2
                value = value[:n] + swap_mem(value[n:], n * 2)
            return value[0]

        back = {}
        early = [0] + near + [last]
        with jax.named_scope("early"):
            summed = reduce_mem(*scores([got[k] for k in [0] + near] + [through, direct], True))
            for at, k in enumerate(early):
                part = summed[:, at * count : (at + 1) * count]
                back[k] = swap(part, k) if k else part
        with jax.named_scope("late"):
            if far:
                summed = reduce_mem(*scores([got[k] for k in far], False))
                for at, k in enumerate(far):
                    back[k] = swap(summed[:, at * count : (at + 1) * count], k)

        with jax.named_scope("coarse"):
            product = lax.dot_general(sketches, rep_sketch, NT, preferred_element_type=f32)
            product = (product * bin_sketch.shape[1] ** (-0.5)).astype(bf)
            each = bin_sketch.shape[0]
            row = iota((product.shape[0], 1), 0) // each
            source = (row % mems ^ mine) * groups + (row // mems ^ me)
            within = iota((product.shape[0], 1), 0) % each
            perm = source * each + within == iota((1, product.shape[0]), 1)
            coarse_scores = pick(perm, product)

        keys = sorted(back)
        with jax.named_scope("final"):
            who = jnp.stack([mine * block] + [me ^ k for k in keys])
            (fine,) = call(
                functools.partial(final_kernel, count, FW ** (-0.5), keys),
                [((2, block, rows_here), f32)], 1, 2 + len(keys), name="final",
            )(who, places, lives, *[back[k] for k in keys])
        return (coarse_scores, fine.transpose(2, 0, 1))

    return local


def solution(mesh):
    return jax.shard_map(
        make_local(mesh.shape["grp"], mesh.shape["mem"]),
        mesh=mesh,
        in_specs=(
            P(("grp", "mem"), None),
            P(("grp", "mem"), None),
            P("grp", "mem"),
            P("grp", None, "mem"),
            P("grp", None),
            P(),
            P(),
        ),
        out_specs=(P(None, ("grp", "mem")), P("grp", None, "mem")),
        check_vma=False,
    )
```

```python
import functools

import jax
import jax.numpy as jnp
from jax import lax
from jax.experimental import pallas as pl
from jax.experimental.pallas import tpu as pltpu
from jax.sharding import PartitionSpec as P


FW = 32768
MOST = 16
VM = pl.BlockSpec(memory_space=pltpu.VMEM)
SM = pl.BlockSpec(memory_space=pltpu.SMEM)
FAR = pl.BlockSpec(memory_space=pltpu.HBM)
NT = (((1,), (1,)), ((), ()))
NN = (((1,), (0,)), ((), ()))


def iota(shape, axis):
    return lax.broadcasted_iota(jnp.int32, shape, axis)


def hits(where, group, count):
    wanted = iota((count, where.shape[1]), 0) + group * count
    return (where[0:1] == wanted) | (where[1:2] == wanted)


def pick(hit, rows):
    one = hit.astype(jnp.float32).astype(jnp.bfloat16)
    return lax.dot_general(one, rows, NN, preferred_element_type=jnp.float32).astype(jnp.bfloat16)


def head_kernel(
    keys, me, slots_far, sizes_far, routes_far, rows_far,
    places, lives, *refs,
):
    outs, (slots, sizes, routes, rows, sems) = refs[: len(keys)], refs[len(keys) :]
    pairs = ((slots_far, slots), (sizes_far, sizes), (routes_far, routes), (rows_far, rows))
    copies = [pltpu.make_async_copy(a, b, sems.at[i]) for i, (a, b) in enumerate(pairs)]
    for copy in copies:
        copy.start()
    total, count = slots.shape[0], outs[0].shape[0]
    width = routes.shape[1]
    before = (iota((width, width), 0) < iota((width, width), 1)).astype(jnp.float32)
    before = before.astype(jnp.bfloat16)
    cluster = iota((total, width), 0)
    slot_of = jnp.zeros((total, width), jnp.int32)
    size_of = jnp.zeros((total, width), jnp.int32)
    for copy in copies[:3]:
        copy.wait()
    for c in range(total):
        slot_of = jnp.where(cluster == c, slots[c], slot_of)
        size_of = jnp.where(cluster == c, sizes[c], size_of)
    seen = jnp.zeros((total, 1), jnp.float32)
    for r in range(2):
        hit = routes[r : r + 1] == cluster
        one = hit.astype(jnp.float32)
        earlier = lax.dot_general(
            one.astype(jnp.bfloat16), before, NN, preferred_element_type=jnp.float32
        )
        rank = jnp.sum(jnp.where(hit, earlier + seen, 0.0), axis=0, keepdims=True)
        seen = seen + jnp.sum(one, axis=1, keepdims=True)
        slot = jnp.sum(jnp.where(hit, slot_of, 0), axis=0, keepdims=True)
        places[r : r + 1] = slot * MOST + rank.astype(jnp.int32)
        lives[r : r + 1] = jnp.sum(jnp.where(hit, size_of, 0), axis=0, keepdims=True)
    where = places[...]
    copies[3].wait()
    for key, out in zip(keys, outs, strict=True):
        out[...] = pick(hits(where, me[0] ^ key, count), rows[...])


def is_inner(me, last):
    return (me[0] == last // 2) | (me[0] == last // 2 + 1)


def forward_kernel(keys, last, me, places_other, whole, *refs):
    outs = refs[len(keys) :]
    count = outs[0].shape[0]

    @pl.when(is_inner(me, last))
    def _():
        where = places_other[...]
        for key, out in zip(keys, outs):
            out[...] = pick(hits(where, me[0] ^ last ^ key, count), whole[...])
        outs[-1][...] = pick(hits(where, me[0], count), whole[...])


def score_kernel(sources, mems, last, lane, me, mine, members, *refs):
    ins, (keep, send, acc) = refs[:sources], refs[-3:]
    slot_count, total, _ = members.shape
    block = total // mems
    count = acc.shape[1]

    def put(src):
        for s in range(slot_count):
            acc[:, s * MOST : (s + 1) * MOST] = lax.dot_general(
                members[s], src[s * MOST : (s + 1) * MOST, :], NT, preferred_element_type=jnp.float32
            )

    if sources == 2:
        inner = is_inner(me, last)

        @pl.when(inner)
        def _():
            put(ins[0])

        @pl.when(jnp.logical_not(inner))
        def _():
            put(ins[1])
    else:
        put(ins[0])
    for p in range(mems // 2):
        for core, out in ((0, keep), (1, send)):
            at = (mine[0] ^ (p * 2 + core)) * block
            out[p, :, lane : lane + count] = acc[pl.ds(pl.multiple_of(at, block), block), :]


def final_kernel(count, scale, keys, me, mine, places, lives, *refs):
    tables, out = refs[:-1], refs[-1]
    block, rows = out.shape[1], out.shape[2]
    member = iota((block, rows), 0) + mine[0] * block
    for r in range(2):
        total = jnp.zeros((block, rows), jnp.float32)
        where = places[r : r + 1]
        for key, table in zip(keys, tables, strict=True):
            wanted = iota((count, rows), 0) + (me[0] ^ key) * count
            one = (where == wanted).astype(jnp.float32)
            total = total + lax.dot_general(
                table[...], one, NN,
                precision=lax.Precision.HIGHEST, preferred_element_type=jnp.float32,
            )
        out[r] = jnp.where(member < lives[r : r + 1], total * scale, 0.0)


def call(kernel, shapes, specs, scratch=(), flops=0, mib=4, alias=()):
    return pl.pallas_call(
        kernel,
        out_shape=[jax.ShapeDtypeStruct(s, d) for s, d in shapes],
        in_specs=specs,
        out_specs=[VM] * len(shapes),
        scratch_shapes=scratch,
        input_output_aliases=dict(alias),
        compiler_params=pltpu.CompilerParams(vmem_limit_bytes=mib << 20),
        cost_estimate=pl.CostEstimate(flops=flops, bytes_accessed=1 << 18, transcendentals=0),
    )


def stay(value):
    return pltpu.with_memory_space_constraint(value, pltpu.HBM)


def make_local(groups, mems):
    last = groups - 1
    half = groups // 2
    middle = (half - 1, half)

    def swap(value, key):
        return lax.ppermute(value, "grp", [(i, i ^ key) for i in range(groups)])

    def swap_mem(value, key):
        return lax.ppermute(value, "mem", [(i, i ^ key) for i in range(mems)])

    def local(
        bin_sketch, rep_sketch, bin_profile, member_profile, bin_routes, owner_slot, cluster_sizes
    ):
        rows_here, width_here = bin_profile.shape
        slot_count, members, _ = member_profile.shape
        count = slot_count * MOST
        block = members // mems
        me = lax.axis_index("grp")
        mine = lax.axis_index("mem")
        me1, mine1 = me.reshape(1), mine.reshape(1)
        member_profile = pltpu.with_memory_space_constraint(member_profile, pltpu.VMEM)
        bf, f32, i32 = jnp.bfloat16, jnp.float32, jnp.int32
        rows_out = ((count, width_here), bf)

        whole = lax.ppermute(bin_profile, "grp", [(i, i ^ last) for i in middle])

        near = list(range(1, half))
        far = list(range(half, last))
        keys = near + [last] + far + [0]
        total = owner_slot.shape[0]
        places, lives, *picked = call(
            functools.partial(head_kernel, keys),
            [((2, rows_here), i32)] * 2 + [rows_out] * len(keys),
            [SM] + [FAR] * 4,
            scratch=[
                pltpu.SMEM((total,), i32), pltpu.SMEM((total,), i32),
                pltpu.VMEM((2, rows_here), i32), pltpu.VMEM(bin_profile.shape, bf),
                pltpu.SemaphoreType.DMA((4,)),
            ],
        )(me1, *[stay(x) for x in (owner_slot, cluster_sizes, bin_routes.T, bin_profile)])
        picked = dict(zip(keys, picked, strict=True))
        places_other = lax.ppermute(places, "grp", [(i, i ^ last) for i in middle])

        sketches = bin_sketch[None]
        sketches = jnp.stack([bin_sketch] + [swap(bin_sketch, k) for k in range(1, groups)])

        got = {0: picked[0]}
        for k in near:
            got[k] = swap(picked[k], k)
        outer = [(i, i ^ last) for i in range(groups) if i not in middle]
        direct = lax.ppermute(picked[last], "grp", outer)
        *onward, through = call(
            functools.partial(forward_kernel, far, last),
            [rows_out] * (len(far) + 1), [SM] + [VM] * (2 + len(far)),
            alias=[(3 + i, i) for i in range(len(far))],
        )(me1, places_other, whole, *[picked[k] for k in far])
        for at, k in enumerate(far):
            way = [(i, i ^ last ^ k if i in middle else i ^ k) for i in range(groups)]
            got[k] = lax.ppermute(onward[at], "grp", way)

        step = 1
        while step < mems:
            sketches = jnp.stack([sketches, swap_mem(sketches, step)])
            step *= 2
        sketches = sketches.reshape(-1, bin_sketch.shape[1])

        def scores(keys):
            shape = ((mems // 2, block, count * len(keys)), f32)
            held = ()
            for at, k in enumerate(keys):
                rows = (through, direct) if k == last else (got[k],)
                held = call(
                    functools.partial(score_kernel, len(rows), mems, last, at * count),
                    [shape] * 2, [SM] * 2 + [VM] * (1 + len(rows) + len(held)),
                    scratch=[pltpu.VMEM((members, count), f32)], mib=2,
                    flops=2 * members * width_here * count * 8,
                    alias=[(3 + len(rows) + i, i) for i in range(len(held))],
                )(me1, mine1, member_profile, *rows, *held)
            return held

        def reduce_mem(keep, send):
            value = keep + swap_mem(send, 1)
            while value.shape[0] > 1:
                n = value.shape[0] // 2
                value = value[:n] + swap_mem(value[n:], n * 2)
            return value[0]

        back = {}
        early = [0] + near + [last]
        summed = reduce_mem(*scores(early))
        for at, k in enumerate(early):
            part = summed[:, at * count : (at + 1) * count]
            back[k] = swap(part, k) if k else part
        if far:
            summed = reduce_mem(*scores(far))
            for at, k in enumerate(far):
                back[k] = swap(summed[:, at * count : (at + 1) * count], k)

        product = lax.dot_general(sketches, rep_sketch, NT, preferred_element_type=f32)
        product = (product * bin_sketch.shape[1] ** (-0.5)).astype(bf)
        each = bin_sketch.shape[0]
        row = iota((product.shape[0], 1), 0) // each
        source = (row % mems ^ mine) * groups + (row // mems ^ me)
        within = iota((product.shape[0], 1), 0) % each
        perm = source * each + within == iota((1, product.shape[0]), 1)
        coarse_scores = pick(perm, product)

        keys = sorted(back)
        (fine,) = call(
            functools.partial(final_kernel, count, FW ** (-0.5), keys),
            [((2, block, rows_here), f32)], [SM] * 2 + [VM] * (2 + len(keys)),
        )(me1, mine1, places, lives, *[back[k] for k in keys])
        return (coarse_scores, fine.transpose(2, 0, 1))

    return local


def solution(mesh):
    local = make_local(mesh.shape["grp"], mesh.shape["mem"])

    return jax.shard_map(
        local,
        mesh=mesh,
        in_specs=(
            P(("grp", "mem"), None),
            P(("grp", "mem"), None),
            P("grp", "mem"),
            P("grp", None, "mem"),
            P("grp", None),
            P(),
            P(),
        ),
        out_specs=(P(None, ("grp", "mem")), P("grp", None, "mem")),
        check_vma=False,
    )
```

```python
import functools

import jax
import jax.numpy as jnp
from jax import lax
from jax.experimental import pallas as pl
from jax.experimental.pallas import tpu as pltpu
from jax.sharding import PartitionSpec as P


FW = 32768
MOST = 16
VM = pl.BlockSpec(memory_space=pltpu.VMEM)
SM = pl.BlockSpec(memory_space=pltpu.SMEM)
FAR = pl.BlockSpec(memory_space=pltpu.HBM)
NT = (((1,), (1,)), ((), ()))
NN = (((1,), (0,)), ((), ()))


def iota(shape, axis):
    return lax.broadcasted_iota(jnp.int32, shape, axis)


def hits(where, group, count):
    wanted = iota((count, where.shape[1]), 0) + group * count
    return (where[0:1] == wanted) | (where[1:2] == wanted)


def pick(hit, rows):
    one = hit.astype(jnp.float32).astype(jnp.bfloat16)
    return lax.dot_general(one, rows, NN, preferred_element_type=jnp.float32).astype(jnp.bfloat16)


def head_kernel(
    keys, me, slots_far, sizes_far, routes_far, rows_far,
    places, lives, *refs,
):
    outs, (slots, sizes, routes, rows, sems) = refs[: len(keys)], refs[len(keys) :]
    pairs = ((slots_far, slots), (sizes_far, sizes), (routes_far, routes), (rows_far, rows))
    copies = [pltpu.make_async_copy(a, b, sems.at[i]) for i, (a, b) in enumerate(pairs)]
    for copy in copies:
        copy.start()
    total, count = slots.shape[0], outs[0].shape[0]
    width = routes.shape[1]
    before = (iota((width, width), 0) < iota((width, width), 1)).astype(jnp.float32)
    before = before.astype(jnp.bfloat16)
    cluster = iota((total, width), 0)
    slot_of = jnp.zeros((total, width), jnp.int32)
    size_of = jnp.zeros((total, width), jnp.int32)
    for copy in copies[:3]:
        copy.wait()
    for c in range(total):
        slot_of = jnp.where(cluster == c, slots[c], slot_of)
        size_of = jnp.where(cluster == c, sizes[c], size_of)
    seen = jnp.zeros((total, 1), jnp.float32)
    for r in range(2):
        hit = routes[r : r + 1] == cluster
        one = hit.astype(jnp.float32)
        earlier = lax.dot_general(
            one.astype(jnp.bfloat16), before, NN, preferred_element_type=jnp.float32
        )
        rank = jnp.sum(jnp.where(hit, earlier + seen, 0.0), axis=0, keepdims=True)
        seen = seen + jnp.sum(one, axis=1, keepdims=True)
        slot = jnp.sum(jnp.where(hit, slot_of, 0), axis=0, keepdims=True)
        places[r : r + 1] = slot * MOST + rank.astype(jnp.int32)
        lives[r : r + 1] = jnp.sum(jnp.where(hit, size_of, 0), axis=0, keepdims=True)
    where = places[...]
    copies[3].wait()
    for key, out in zip(keys, outs, strict=True):
        out[...] = pick(hits(where, me[0] ^ key, count), rows[...])


def is_inner(me, last):
    return (me[0] == last // 2) | (me[0] == last // 2 + 1)


def forward_kernel(keys, last, me, places_other, whole, *refs):
    outs = refs[len(keys) :]
    count = outs[0].shape[0]

    @pl.when(is_inner(me, last))
    def _():
        where = places_other[...]
        for key, out in zip(keys, outs):
            out[...] = pick(hits(where, me[0] ^ last ^ key, count), whole[...])
        outs[-1][...] = pick(hits(where, me[0], count), whole[...])


def score_kernel(keys, last, me, core, members, *refs):
    keep, send, acc = refs[-3:]
    ins = list(refs[: len(keys) + (last in keys)])
    slot_count, total, _ = members.shape
    chips = keep.shape[1]
    block = total // (2 * chips)

    def put(ins):
        for s in range(slot_count):
            rows = [src[s * MOST : (s + 1) * MOST, :] for src in ins]
            rows = jnp.concatenate(rows, axis=0) if len(rows) > 1 else rows[0]
            product = lax.dot_general(members[s], rows, NT, preferred_element_type=jnp.float32)
            acc[s] = product.T

    def give(first, second):
        for at, key in enumerate(keys):
            for chip in range(chips):
                for side, out in enumerate((first, second)):
                    start = (chip * 2 + side) * block
                    for s in range(slot_count):
                        out[me[0] ^ key, chip, :, s * block : (s + 1) * block] = (
                            acc[s, at * MOST : (at + 1) * MOST, start : start + block]
                        )

    if last in keys:
        inner = is_inner(me, last)
        pl.when(inner)(lambda: put(ins[:-1]))
        pl.when(jnp.logical_not(inner))(lambda: put(ins[:-2] + ins[-1:]))
    else:
        put(ins)
    pl.when(core[0] == 0)(lambda: give(keep, send))
    pl.when(core[0] == 1)(lambda: give(send, keep))


def gate_kernel(members, rows, out):
    out[0:16, 0:128] = rows[0:16, 0:128]


def half_kernel(key, other, me, core, members, rows, _, out, acc):
    slot_count, chips = members.shape[0], out.shape[1]
    block = members.shape[1] // (2 * chips)
    starts = [pl.multiple_of((chip * 2 + (core[0] ^ other)) * block, block) for chip in range(chips)]
    for s in range(slot_count):
        half = jnp.concatenate([members[s, pl.ds(start, block), :] for start in starts], axis=0)
        product = lax.dot_general(
            half, rows[s * MOST : (s + 1) * MOST, :], NT, preferred_element_type=jnp.float32
        )
        acc[...] = product.T
        for chip in range(chips):
            out[me[0] ^ key, chip, :, s * block : (s + 1) * block] = (
                acc[:, chip * block : (chip + 1) * block]
            )


def final_kernel(slot_count, scale, mine, places, lives, parts, out):
    groups, chips = parts.shape[:2]
    block, rows = out.shape[1], out.shape[2]
    member = iota((block, rows), 0) + mine[0] * block
    tables = []
    for group in range(groups):
        total = parts[group, 0]
        for chip in range(1, chips):
            total = total + parts[group, chip]
        for s in range(slot_count):
            tables.append(total[:, s * block : (s + 1) * block])
    table = jnp.concatenate(tables, axis=0)
    for r in range(2):
        one = (places[r : r + 1] == iota((table.shape[0], rows), 0)).astype(jnp.float32)
        score = lax.dot_general(
            table, one, (((0,), (0,)), ((), ())),
            precision=lax.Precision.HIGHEST, preferred_element_type=jnp.float32,
        )
        out[r] = jnp.where(member < lives[r : r + 1], score * scale, 0.0)


def call(kernel, shapes, specs, scratch=(), flops=0, mib=4, alias=()):
    return pl.pallas_call(
        kernel,
        out_shape=[jax.ShapeDtypeStruct(s, d) for s, d in shapes],
        in_specs=specs,
        out_specs=[VM] * len(shapes),
        scratch_shapes=scratch,
        input_output_aliases=dict(alias),
        compiler_params=pltpu.CompilerParams(vmem_limit_bytes=mib << 20),
        cost_estimate=pl.CostEstimate(flops=flops, bytes_accessed=1 << 18, transcendentals=0),
    )


def stay(value):
    return pltpu.with_memory_space_constraint(value, pltpu.HBM)


def make_local(groups, chips):
    last = groups - 1
    half = groups // 2
    middle = (half - 1, half)
    mems = 2 * chips

    def swap(value, key):
        return lax.ppermute(value, "grp", [(i, i ^ key) for i in range(groups)])

    def swap_mem(value, key):
        if key == 1:
            return lax.ppermute(value, "core", [(0, 1), (1, 0)])
        return lax.ppermute(value, "chip", [(i, i ^ (key // 2)) for i in range(chips)])

    def local(
        bin_sketch, rep_sketch, bin_profile, member_profile, bin_routes, owner_slot, cluster_sizes
    ):
        rows_here, width_here = bin_profile.shape
        slot_count, members, _ = member_profile.shape
        count = slot_count * MOST
        block = members // mems
        me = lax.axis_index("grp")
        core = lax.axis_index("core")
        mine = lax.axis_index("chip") * 2 + core
        member_profile = pltpu.with_memory_space_constraint(member_profile, pltpu.VMEM)
        me1, mine1, core1 = me.reshape(1), mine.reshape(1), core.reshape(1)
        bf, f32, i32 = jnp.bfloat16, jnp.float32, jnp.int32
        rows_out = ((count, width_here), bf)

        whole = lax.ppermute(bin_profile, "grp", [(i, i ^ last) for i in middle])

        near = list(range(1, half))
        far = list(range(half, last))
        keys = near + [last] + far + [0]
        total = owner_slot.shape[0]
        places, lives, *picked = call(
            functools.partial(head_kernel, keys),
            [((2, rows_here), i32)] * 2 + [rows_out] * len(keys),
            [SM] + [FAR] * 4,
            scratch=[
                pltpu.SMEM((total,), i32), pltpu.SMEM((total,), i32),
                pltpu.VMEM((2, rows_here), i32), pltpu.VMEM(bin_profile.shape, bf),
                pltpu.SemaphoreType.DMA((4,)),
            ],
        )(me1, *[stay(x) for x in (owner_slot, cluster_sizes, bin_routes.T, bin_profile)])
        picked = dict(zip(keys, picked, strict=True))
        places_other = lax.ppermute(places, "grp", [(i, i ^ last) for i in middle])

        sketches = bin_sketch[None]
        step = 1
        while step < groups:
            sketches = jnp.concatenate([sketches, swap(sketches, step)])
            step *= 2

        got = {0: picked[0]}
        for k in near:
            got[k] = swap(picked[k], k)
        outer = [(i, i ^ last) for i in range(groups) if i not in middle]
        (rows,) = call(
            gate_kernel, [rows_out], [VM] * 2, mib=2, alias=[(1, 0)]
        )(member_profile, picked[last])
        direct = lax.ppermute(rows, "grp", outer)
        *onward, through = call(
            functools.partial(forward_kernel, far, last),
            [rows_out] * (len(far) + 1), [SM] + [VM] * (2 + len(far)),
            alias=[(3 + i, i) for i in range(len(far))],
        )(me1, places_other, whole, *[picked[k] for k in far])
        for at, k in enumerate(far):
            way = [(i, i ^ last ^ k if i in middle else i ^ k) for i in range(groups)]
            got[k] = lax.ppermute(onward[at], "grp", way)

        step = 1
        while step < mems:
            sketches = jnp.stack([sketches, swap_mem(sketches, step)])
            step *= 2
        sketches = sketches.reshape(-1, bin_sketch.shape[1])

        shape = ((groups, chips, MOST, 128), f32)
        held = ()
        got[last] = through
        for keys in ([0] + near + [last],):
            rows = [got[k] for k in keys] + ([direct] if last in keys else [])
            held = call(
                functools.partial(score_kernel, keys, last), [shape] * 2,
                [SM] * 2 + [VM] * (1 + len(rows) + len(held)),
                scratch=[pltpu.VMEM((slot_count, MOST * len(keys), members), f32)],
                mib=2,
                flops=2 * members * width_here * count * 8,
                alias=[(3 + len(rows) + i, i) for i in range(len(held))],
            )(me1, core1, member_profile, *rows, *held)
        keep, send = held

        def one_side(key, other, out):
            (out,) = call(
                functools.partial(half_kernel, key, other), [shape], [SM] * 2 + [VM] * 3,
                scratch=[pltpu.VMEM((MOST, members // 2), f32)], mib=2,
                flops=members * width_here * count * 8, alias=[(4, 0)],
            )(me1, core1, member_profile, got[key], out)
            return out

        for k in far:
            send = one_side(k, 1, send)
        send = swap_mem(send, 1)
        for k in far:
            keep = one_side(k, 0, keep)
        parts = keep + send
        parts = parts.reshape(groups * chips, MOST, 128)
        parts = lax.all_to_all(parts, ("grp", "chip"), 0, 0, tiled=True)
        parts = parts.reshape(groups, chips, MOST, 128)

        product = lax.dot_general(sketches, rep_sketch, NT, preferred_element_type=f32)
        product = (product * bin_sketch.shape[1] ** (-0.5)).astype(bf)
        each = bin_sketch.shape[0]
        row = iota((product.shape[0], 1), 0) // each
        source = (row % mems ^ mine) * groups + (row // mems ^ me)
        within = iota((product.shape[0], 1), 0) % each
        perm = source * each + within == iota((1, product.shape[0]), 1)
        coarse_scores = pick(perm, product)

        (fine,) = call(
            functools.partial(final_kernel, slot_count, FW ** (-0.5)),
            [((2, block, rows_here), f32)], [SM] + [VM] * 3,
        )(mine1, places, lives, parts)
        return (coarse_scores, fine.transpose(2, 0, 1))

    return local


def solution(mesh):
    groups, chips = mesh.shape["grp"], mesh.shape["mem"] // 2
    mesh = jax.sharding.Mesh(mesh.devices.reshape(groups, chips, 2), ("grp", "chip", "core"))
    mem = ("chip", "core")
    local = make_local(groups, chips)

    return jax.shard_map(
        local,
        mesh=mesh,
        in_specs=(
            P(("grp", *mem), None),
            P(("grp", *mem), None),
            P("grp", mem),
            P("grp", None, mem),
            P("grp", None),
            P(),
            P(),
        ),
        out_specs=(P(None, ("grp", *mem)), P("grp", None, mem)),
        check_vma=False,
    )
```

```python
import functools

import jax
import jax.numpy as jnp
from jax import lax
from jax.experimental import pallas as pl
from jax.experimental.pallas import tpu as pltpu
from jax.sharding import PartitionSpec as P


FW = 32768
MOST = 16
VM = pl.BlockSpec(memory_space=pltpu.VMEM)
SM = pl.BlockSpec(memory_space=pltpu.SMEM)
FAR = pl.BlockSpec(memory_space=pltpu.HBM)
NT = (((1,), (1,)), ((), ()))
NN = (((1,), (0,)), ((), ()))


def iota(shape, axis):
    return lax.broadcasted_iota(jnp.int32, shape, axis)


def hits(where, group, count):
    wanted = iota((count, where.shape[1]), 0) + group * count
    return (where[0:1] == wanted) | (where[1:2] == wanted)


def pick(hit, rows):
    one = hit.astype(jnp.float32).astype(jnp.bfloat16)
    return lax.dot_general(one, rows, NN, preferred_element_type=jnp.float32).astype(jnp.bfloat16)


def head_kernel(
    keys, slot_count, me, slots_far, sizes_far, routes_far, rows_far,
    places, lives, lines, slots_in, *refs,
):
    outs, (slots, sizes, routes, rows, sems) = refs[: len(keys)], refs[len(keys) :]
    pairs = ((slots_far, slots), (sizes_far, sizes), (routes_far, routes), (rows_far, rows))
    copies = [pltpu.make_async_copy(a, b, sems.at[i]) for i, (a, b) in enumerate(pairs)]
    for copy in copies:
        copy.start()
    total, count = slots.shape[0], outs[0].shape[0]
    width = routes.shape[1]
    before = (iota((width, width), 0) < iota((width, width), 1)).astype(jnp.float32)
    before = before.astype(jnp.bfloat16)
    cluster = iota((total, width), 0)
    slot_of = jnp.zeros((total, width), jnp.int32)
    size_of = jnp.zeros((total, width), jnp.int32)
    group_of = jnp.zeros((total, width), jnp.int32)
    for copy in copies[:3]:
        copy.wait()
    for c in range(total):
        slot_of = jnp.where(cluster == c, slots[c], slot_of)
        size_of = jnp.where(cluster == c, sizes[c], size_of)
        group_of = jnp.where(cluster == c, slots[c] // slot_count, group_of)
    seen = jnp.zeros((total, 1), jnp.float32)
    for r in range(2):
        hit = routes[r : r + 1] == cluster
        one = hit.astype(jnp.float32)
        earlier = lax.dot_general(
            one.astype(jnp.bfloat16), before, NN, preferred_element_type=jnp.float32
        )
        rank = jnp.sum(jnp.where(hit, earlier + seen, 0.0), axis=0, keepdims=True)
        seen = seen + jnp.sum(one, axis=1, keepdims=True)
        slot = jnp.sum(jnp.where(hit, slot_of, 0), axis=0, keepdims=True)
        group = jnp.sum(jnp.where(hit, group_of, 0), axis=0, keepdims=True)
        places[r : r + 1] = slot * MOST + rank.astype(jnp.int32)
        lines[r : r + 1] = group * MOST + rank.astype(jnp.int32)
        slots_in[r : r + 1] = slot - group * slot_count
        lives[r : r + 1] = jnp.sum(jnp.where(hit, size_of, 0), axis=0, keepdims=True)
    where = places[...]
    copies[3].wait()
    for key, out in zip(keys, outs, strict=True):
        out[...] = pick(hits(where, me[0] ^ key, count), rows[...])


def is_inner(me, last):
    return (me[0] == last // 2) | (me[0] == last // 2 + 1)


def forward_kernel(keys, last, me, places_other, whole, *refs):
    outs = refs[len(keys) :]
    count = outs[0].shape[0]

    @pl.when(is_inner(me, last))
    def _():
        where = places_other[...]
        for key, out in zip(keys, outs):
            out[...] = pick(hits(where, me[0] ^ last ^ key, count), whole[...])
        outs[-1][...] = pick(hits(where, me[0], count), whole[...])


def score_kernel(keys, last, me, core, members, *refs):
    keep, send, acc = refs[-3:]
    ins = list(refs[: len(keys) + (last in keys)])
    slot_count, total, _ = members.shape
    chips = keep.shape[1]
    block = total // (2 * chips)

    def put(ins):
        for s in range(slot_count):
            rows = [src[s * MOST : (s + 1) * MOST, :] for src in ins]
            rows = jnp.concatenate(rows, axis=0) if len(rows) > 1 else rows[0]
            product = lax.dot_general(members[s], rows, NT, preferred_element_type=jnp.float32)
            acc[s] = product.T

    def give(first, second):
        for at, key in enumerate(keys):
            for chip in range(chips):
                for side, out in enumerate((first, second)):
                    start = (chip * 2 + side) * block
                    for s in range(slot_count):
                        out[me[0] ^ key, chip, :, s * block : (s + 1) * block] = (
                            acc[s, at * MOST : (at + 1) * MOST, start : start + block]
                        )

    if last in keys:
        inner = is_inner(me, last)
        pl.when(inner)(lambda: put(ins[:-1]))
        pl.when(jnp.logical_not(inner))(lambda: put(ins[:-2] + ins[-1:]))
    else:
        put(ins)
    pl.when(core[0] == 0)(lambda: give(keep, send))
    pl.when(core[0] == 1)(lambda: give(send, keep))


def gate_kernel(members, rows, out):
    out[0:16, 0:128] = rows[0:16, 0:128]


def coarse_kernel(scale, me, mine, reps, *refs):
    parts, out = refs[:-1], refs[-1]
    cores, groups, each, width = parts[0].shape
    mems = cores * len(parts)
    lines = cores * groups
    batch = max(1, 256 // (lines * each))
    for first in range(0, len(parts), batch):
        rows = [part[...].reshape(lines * each, width) for part in parts[first : first + batch]]
        rows = jnp.concatenate(rows, axis=0) if len(rows) > 1 else rows[0]
        score = lax.dot_general(rows, reps[...], NT, preferred_element_type=jnp.float32)
        score = (score * scale).astype(out.dtype)
        for at in range(score.shape[0] // each):
            member = mine[0] ^ (first * cores + at // groups)
            out[(me[0] ^ (at % groups)) * mems + member] = score[at * each : (at + 1) * each]


def half_kernel(key, other, me, core, members, rows, _, out, acc):
    slot_count, chips = members.shape[0], out.shape[1]
    block = members.shape[1] // (2 * chips)
    starts = [pl.multiple_of((chip * 2 + (core[0] ^ other)) * block, block) for chip in range(chips)]
    for s in range(slot_count):
        half = jnp.concatenate([members[s, pl.ds(start, block), :] for start in starts], axis=0)
        product = lax.dot_general(
            half, rows[s * MOST : (s + 1) * MOST, :], NT, preferred_element_type=jnp.float32
        )
        acc[...] = product.T
        for chip in range(chips):
            out[me[0] ^ key, chip, :, s * block : (s + 1) * block] = (
                acc[:, chip * block : (chip + 1) * block]
            )


def final_kernel(slot_count, scale, mine, lines, slots, lives, parts, out):
    groups, chips = parts.shape[:2]
    block, rows = out.shape[1], out.shape[2]
    member = iota((block, rows), 0) + mine[0] * block
    total = parts[:, 0]
    for chip in range(1, chips):
        total = total + parts[:, chip]
    total = total.reshape(groups * MOST, total.shape[2])
    line = jnp.concatenate([lines[r : r + 1] for r in range(2)], axis=1)
    one = (line == iota((groups * MOST, 2 * rows), 0)).astype(jnp.float32).astype(jnp.bfloat16)
    score = jnp.zeros((total.shape[1], 2 * rows), jnp.float32)
    for _ in range(3):
        piece = total.astype(jnp.bfloat16)
        total = total - piece.astype(jnp.float32)
        score = score + lax.dot_general(
            piece, one, (((0,), (0,)), ((), ())), preferred_element_type=jnp.float32
        )
    for r in range(2):
        slot = slots[r : r + 1]
        found = jnp.zeros((block, rows), jnp.float32)
        for s in range(slot_count):
            part = score[s * block : (s + 1) * block, r * rows : (r + 1) * rows]
            found = jnp.where(slot == s, part, found)
        out[r] = jnp.where(member < lives[r : r + 1], found * scale, 0.0)


def call(kernel, shapes, specs, scratch=(), flops=0, mib=4, alias=()):
    return pl.pallas_call(
        kernel,
        out_shape=[jax.ShapeDtypeStruct(s, d) for s, d in shapes],
        in_specs=specs,
        out_specs=[VM] * len(shapes),
        scratch_shapes=scratch,
        input_output_aliases=dict(alias),
        compiler_params=pltpu.CompilerParams(vmem_limit_bytes=mib << 20),
        cost_estimate=pl.CostEstimate(flops=flops, bytes_accessed=1 << 18, transcendentals=0),
    )


def stay(value):
    return pltpu.with_memory_space_constraint(value, pltpu.HBM)


def make_local(groups, chips):
    last = groups - 1
    half = groups // 2
    middle = (half - 1, half)
    mems = 2 * chips

    def swap(value, key):
        return lax.ppermute(value, "grp", [(i, i ^ key) for i in range(groups)])

    def swap_mem(value, key):
        if key == 1:
            return lax.ppermute(value, "core", [(0, 1), (1, 0)])
        return lax.ppermute(value, "chip", [(i, i ^ (key // 2)) for i in range(chips)])

    def local(
        bin_sketch, rep_sketch, bin_profile, member_profile, bin_routes, owner_slot, cluster_sizes
    ):
        rows_here, width_here = bin_profile.shape
        slot_count, members, _ = member_profile.shape
        count = slot_count * MOST
        block = members // mems
        me = lax.axis_index("grp")
        core = lax.axis_index("core")
        mine = lax.axis_index("chip") * 2 + core
        member_profile = pltpu.with_memory_space_constraint(member_profile, pltpu.VMEM)
        me1, mine1, core1 = me.reshape(1), mine.reshape(1), core.reshape(1)
        bf, f32, i32 = jnp.bfloat16, jnp.float32, jnp.int32
        rows_out = ((count, width_here), bf)

        whole = lax.ppermute(bin_profile, "grp", [(i, i ^ last) for i in middle])

        near = list(range(1, half))
        far = list(range(half, last))
        keys = near + [last] + far + [0]
        total = owner_slot.shape[0]
        places, lives, lines, slots_in, *picked = call(
            functools.partial(head_kernel, keys, slot_count),
            [((2, rows_here), i32)] * 4 + [rows_out] * len(keys),
            [SM] + [FAR] * 4,
            scratch=[
                pltpu.SMEM((total,), i32), pltpu.SMEM((total,), i32),
                pltpu.VMEM((2, rows_here), i32), pltpu.VMEM(bin_profile.shape, bf),
                pltpu.SemaphoreType.DMA((4,)),
            ],
        )(me1, *[stay(x) for x in (owner_slot, cluster_sizes, bin_routes.T, bin_profile)])
        picked = dict(zip(keys, picked, strict=True))
        places_other = lax.ppermute(places, "grp", [(i, i ^ last) for i in middle])

        sketches = bin_sketch[None]
        step = 1
        while step < groups:
            sketches = jnp.concatenate([sketches, swap(sketches, step)])
            step *= 2

        got = {0: picked[0]}
        for k in near:
            got[k] = swap(picked[k], k)
        outer = [(i, i ^ last) for i in range(groups) if i not in middle]
        (rows,) = call(
            gate_kernel, [rows_out], [VM] * 2, mib=2, alias=[(1, 0)]
        )(member_profile, picked[last])
        direct = lax.ppermute(rows, "grp", outer)
        *onward, through = call(
            functools.partial(forward_kernel, far, last),
            [rows_out] * (len(far) + 1), [SM] + [VM] * (2 + len(far)),
            alias=[(3 + i, i) for i in range(len(far))],
        )(me1, places_other, whole, *[picked[k] for k in far])
        for at, k in enumerate(far):
            way = [(i, i ^ last ^ k if i in middle else i ^ k) for i in range(groups)]
            got[k] = lax.ppermute(onward[at], "grp", way)

        sketches = jnp.stack([sketches, swap_mem(sketches, 1)]).reshape(2, groups, *bin_sketch.shape)
        parts = [sketches]
        for q in range(1, chips):
            parts.append(swap_mem(sketches, 2 * q))
        each = bin_sketch.shape[0]
        (coarse,) = call(
            functools.partial(coarse_kernel, bin_sketch.shape[1] ** (-0.5)),
            [((groups * mems, each, rep_sketch.shape[0]), bf)],
            [SM] * 2 + [VM] * (1 + chips), mib=40 if groups * mems > 256 else 4,
            flops=2 * groups * mems * each * rep_sketch.size,
        )(me1, mine1, rep_sketch, *parts)
        coarse_scores = coarse.reshape(-1, rep_sketch.shape[0])

        shape = ((groups, chips, MOST, 128), f32)
        held = ()
        got[last] = through
        for keys in ([0], near + [last]):
            rows = [got[k] for k in keys] + ([direct] if last in keys else [])
            held = call(
                functools.partial(score_kernel, keys, last), [shape] * 2,
                [SM] * 2 + [VM] * (1 + len(rows) + len(held)),
                scratch=[pltpu.VMEM((slot_count, MOST * len(keys), members), f32)],
                mib=2,
                flops=2 * members * width_here * count * 8,
                alias=[(3 + len(rows) + i, i) for i in range(len(held))],
            )(me1, core1, member_profile, *rows, *held)
        keep, send = held

        def one_side(key, other, out):
            (out,) = call(
                functools.partial(half_kernel, key, other), [shape], [SM] * 2 + [VM] * 3,
                scratch=[pltpu.VMEM((MOST, members // 2), f32)], mib=2,
                flops=members * width_here * count * 8, alias=[(4, 0)],
            )(me1, core1, member_profile, got[key], out)
            return out

        for k in far:
            send = one_side(k, 1, send)
        send = swap_mem(send, 1)
        for k in far:
            keep = one_side(k, 0, keep)
        parts = keep + send
        parts = parts.reshape(groups * chips, MOST, 128)
        parts = lax.all_to_all(parts, ("grp", "chip"), 0, 0, tiled=True)
        parts = parts.reshape(groups, chips, MOST, 128)

        (fine,) = call(
            functools.partial(final_kernel, slot_count, FW ** (-0.5)),
            [((2, block, rows_here), f32)], [SM] + [VM] * 4,
        )(mine1, lines, slots_in, lives, parts)
        return (coarse_scores, fine.transpose(2, 0, 1))

    return local


def solution(mesh):
    groups, chips = mesh.shape["grp"], mesh.shape["mem"] // 2
    mesh = jax.sharding.Mesh(mesh.devices.reshape(groups, chips, 2), ("grp", "chip", "core"))
    mem = ("chip", "core")
    local = make_local(groups, chips)

    return jax.shard_map(
        local,
        mesh=mesh,
        in_specs=(
            P(("grp", *mem), None),
            P(("grp", *mem), None),
            P("grp", mem),
            P("grp", None, mem),
            P("grp", None),
            P(),
            P(),
        ),
        out_specs=(P(None, ("grp", *mem)), P("grp", None, mem)),
        check_vma=False,
    )
```

```python
import functools

import jax
import jax.numpy as jnp
from jax import lax
from jax.experimental import pallas as pl
from jax.experimental.pallas import tpu as pltpu
from jax.sharding import PartitionSpec as P


FW = 32768
MOST = 16
VM = pl.BlockSpec(memory_space=pltpu.VMEM)
SM = pl.BlockSpec(memory_space=pltpu.SMEM)
FAR = pl.BlockSpec(memory_space=pltpu.HBM)
NT = (((1,), (1,)), ((), ()))
NN = (((1,), (0,)), ((), ()))


def iota(shape, axis):
    return lax.broadcasted_iota(jnp.int32, shape, axis)


def hits(where, group, count):
    wanted = iota((count, where.shape[1]), 0) + group * count
    return (where[0:1] == wanted) | (where[1:2] == wanted)


def pick(hit, rows):
    one = hit.astype(jnp.float32).astype(jnp.bfloat16)
    return lax.dot_general(one, rows, NN, preferred_element_type=jnp.float32).astype(jnp.bfloat16)


def head_kernel(
    keys, slot_count, me, slots_far, sizes_far, routes_far, rows_far,
    places, lives, lines, slots_in, *refs,
):
    outs, (slots, sizes, routes, rows, sems) = refs[: len(keys)], refs[len(keys) :]
    pairs = ((slots_far, slots), (sizes_far, sizes), (routes_far, routes), (rows_far, rows))
    copies = [pltpu.make_async_copy(a, b, sems.at[i]) for i, (a, b) in enumerate(pairs)]
    for copy in copies:
        copy.start()
    total, count = slots.shape[0], outs[0].shape[0]
    width = routes.shape[1]
    before = (iota((width, width), 0) < iota((width, width), 1)).astype(jnp.float32)
    before = before.astype(jnp.bfloat16)
    cluster = iota((total, width), 0)
    slot_of = jnp.zeros((total, width), jnp.int32)
    size_of = jnp.zeros((total, width), jnp.int32)
    group_of = jnp.zeros((total, width), jnp.int32)
    for copy in copies[:3]:
        copy.wait()
    for c in range(total):
        slot_of = jnp.where(cluster == c, slots[c], slot_of)
        size_of = jnp.where(cluster == c, sizes[c], size_of)
        group_of = jnp.where(cluster == c, slots[c] // slot_count, group_of)
    seen = jnp.zeros((total, 1), jnp.float32)
    for r in range(2):
        hit = routes[r : r + 1] == cluster
        one = hit.astype(jnp.float32)
        earlier = lax.dot_general(
            one.astype(jnp.bfloat16), before, NN, preferred_element_type=jnp.float32
        )
        rank = jnp.sum(jnp.where(hit, earlier + seen, 0.0), axis=0, keepdims=True)
        seen = seen + jnp.sum(one, axis=1, keepdims=True)
        slot = jnp.sum(jnp.where(hit, slot_of, 0), axis=0, keepdims=True)
        group = jnp.sum(jnp.where(hit, group_of, 0), axis=0, keepdims=True)
        places[r : r + 1] = slot * MOST + rank.astype(jnp.int32)
        lines[r : r + 1] = group * MOST + rank.astype(jnp.int32)
        slots_in[r : r + 1] = slot - group * slot_count
        lives[r : r + 1] = jnp.sum(jnp.where(hit, size_of, 0), axis=0, keepdims=True)
    where = places[...]
    copies[3].wait()
    for key, out in zip(keys, outs, strict=True):
        out[...] = pick(hits(where, me[0] ^ key, count), rows[...])


def is_inner(me, last):
    return (me[0] == last // 2) | (me[0] == last // 2 + 1)


def forward_kernel(keys, last, me, places_other, whole, *refs):
    outs = refs[len(keys) :]
    count = outs[0].shape[0]

    @pl.when(is_inner(me, last))
    def _():
        where = places_other[...]
        for key, out in zip(keys, outs):
            out[...] = pick(hits(where, me[0] ^ last ^ key, count), whole[...])
        outs[-1][...] = pick(hits(where, me[0], count), whole[...])


def score_kernel(keys, last, me, core, members, *refs):
    keep, send, acc = refs[-3:]
    ins = list(refs[: len(keys) + (last in keys)])
    slot_count, total, _ = members.shape
    chips = keep.shape[1]
    block = total // (2 * chips)

    def put(ins):
        for s in range(slot_count):
            rows = [src[s * MOST : (s + 1) * MOST, :] for src in ins]
            rows = jnp.concatenate(rows, axis=0) if len(rows) > 1 else rows[0]
            product = lax.dot_general(members[s], rows, NT, preferred_element_type=jnp.float32)
            acc[s] = product.T

    def give(first, second):
        for at, key in enumerate(keys):
            for chip in range(chips):
                for side, out in enumerate((first, second)):
                    start = (chip * 2 + side) * block
                    for s in range(slot_count):
                        out[me[0] ^ key, chip, :, s * block : (s + 1) * block] = (
                            acc[s, at * MOST : (at + 1) * MOST, start : start + block]
                        )

    if last in keys:
        inner = is_inner(me, last)
        pl.when(inner)(lambda: put(ins[:-1]))
        pl.when(jnp.logical_not(inner))(lambda: put(ins[:-2] + ins[-1:]))
    else:
        put(ins)
    pl.when(core[0] == 0)(lambda: give(keep, send))
    pl.when(core[0] == 1)(lambda: give(send, keep))


def coarse_kernel(scale, me, mine, reps, *refs):
    parts, out = refs[:-1], refs[-1]
    cores, groups, each, width = parts[0].shape
    mems = cores * len(parts)
    lines = cores * groups
    batch = max(1, 256 // (lines * each))
    for first in range(0, len(parts), batch):
        rows = [part[...].reshape(lines * each, width) for part in parts[first : first + batch]]
        rows = jnp.concatenate(rows, axis=0) if len(rows) > 1 else rows[0]
        score = lax.dot_general(rows, reps[...], NT, preferred_element_type=jnp.float32)
        score = (score * scale).astype(out.dtype)
        for at in range(score.shape[0] // each):
            member = mine[0] ^ (first * cores + at // groups)
            out[(me[0] ^ (at % groups)) * mems + member] = score[at * each : (at + 1) * each]


def half_kernel(key, other, me, core, members, rows, _, out, acc):
    slot_count, chips = members.shape[0], out.shape[1]
    block = members.shape[1] // (2 * chips)
    starts = [pl.multiple_of((chip * 2 + (core[0] ^ other)) * block, block) for chip in range(chips)]
    for s in range(slot_count):
        half = jnp.concatenate([members[s, pl.ds(start, block), :] for start in starts], axis=0)
        product = lax.dot_general(
            half, rows[s * MOST : (s + 1) * MOST, :], NT, preferred_element_type=jnp.float32
        )
        acc[...] = product.T
        for chip in range(chips):
            out[me[0] ^ key, chip, :, s * block : (s + 1) * block] = (
                acc[:, chip * block : (chip + 1) * block]
            )


def final_kernel(slot_count, scale, mine, lines, slots, lives, parts, out):
    groups, chips = parts.shape[:2]
    block, rows = out.shape[1], out.shape[2]
    member = iota((block, rows), 0) + mine[0] * block
    total = parts[:, 0]
    for chip in range(1, chips):
        total = total + parts[:, chip]
    total = total.reshape(groups * MOST, total.shape[2])
    line = jnp.concatenate([lines[r : r + 1] for r in range(2)], axis=1)
    one = (line == iota((groups * MOST, 2 * rows), 0)).astype(jnp.float32).astype(jnp.bfloat16)
    score = jnp.zeros((total.shape[1], 2 * rows), jnp.float32)
    for _ in range(3):
        piece = total.astype(jnp.bfloat16)
        total = total - piece.astype(jnp.float32)
        score = score + lax.dot_general(
            piece, one, (((0,), (0,)), ((), ())), preferred_element_type=jnp.float32
        )
    for r in range(2):
        slot = slots[r : r + 1]
        found = jnp.zeros((block, rows), jnp.float32)
        for s in range(slot_count):
            part = score[s * block : (s + 1) * block, r * rows : (r + 1) * rows]
            found = jnp.where(slot == s, part, found)
        out[r] = jnp.where(member < lives[r : r + 1], found * scale, 0.0)


def call(kernel, shapes, specs, scratch=(), flops=0, mib=4, alias=()):
    return pl.pallas_call(
        kernel,
        out_shape=[jax.ShapeDtypeStruct(s, d) for s, d in shapes],
        in_specs=specs,
        out_specs=[VM] * len(shapes),
        scratch_shapes=scratch,
        input_output_aliases=dict(alias),
        compiler_params=pltpu.CompilerParams(vmem_limit_bytes=mib << 20),
        cost_estimate=pl.CostEstimate(flops=flops, bytes_accessed=1 << 18, transcendentals=0),
    )


def stay(value):
    return pltpu.with_memory_space_constraint(value, pltpu.HBM)


def make_local(groups, chips):
    last = groups - 1
    half = groups // 2
    middle = (half - 1, half)
    mems = 2 * chips

    def swap(value, key):
        return lax.ppermute(value, "grp", [(i, i ^ key) for i in range(groups)])

    def swap_mem(value, key):
        if key == 1:
            return lax.ppermute(value, "core", [(0, 1), (1, 0)])
        return lax.ppermute(value, "chip", [(i, i ^ (key // 2)) for i in range(chips)])

    def local(
        bin_sketch, rep_sketch, bin_profile, member_profile, bin_routes, owner_slot, cluster_sizes
    ):
        rows_here, width_here = bin_profile.shape
        slot_count, members, _ = member_profile.shape
        count = slot_count * MOST
        block = members // mems
        me = lax.axis_index("grp")
        core = lax.axis_index("core")
        mine = lax.axis_index("chip") * 2 + core
        member_profile = pltpu.with_memory_space_constraint(member_profile, pltpu.VMEM)
        me1, mine1, core1 = me.reshape(1), mine.reshape(1), core.reshape(1)
        bf, f32, i32 = jnp.bfloat16, jnp.float32, jnp.int32
        rows_out = ((count, width_here), bf)

        whole = lax.ppermute(bin_profile, "grp", [(i, i ^ last) for i in middle])

        near = list(range(1, half))
        far = list(range(half, last))
        keys = near + [last] + far + [0]
        total = owner_slot.shape[0]
        places, lives, lines, slots_in, *picked = call(
            functools.partial(head_kernel, keys, slot_count),
            [((2, rows_here), i32)] * 4 + [rows_out] * len(keys),
            [SM] + [FAR] * 4,
            scratch=[
                pltpu.SMEM((total,), i32), pltpu.SMEM((total,), i32),
                pltpu.VMEM((2, rows_here), i32), pltpu.VMEM(bin_profile.shape, bf),
                pltpu.SemaphoreType.DMA((4,)),
            ],
        )(me1, *[stay(x) for x in (owner_slot, cluster_sizes, bin_routes.T, bin_profile)])
        picked = dict(zip(keys, picked, strict=True))
        places_other = lax.ppermute(places, "grp", [(i, i ^ last) for i in middle])

        sketches = bin_sketch[None]
        step = 1
        while step < groups:
            sketches = jnp.concatenate([sketches, swap(sketches, step)])
            step *= 2

        got = {0: picked[0]}
        for k in near:
            got[k] = swap(picked[k], k)
        outer = [(i, i ^ last) for i in range(groups) if i not in middle]
        direct = lax.ppermute(picked[last], "grp", outer)
        *onward, through = call(
            functools.partial(forward_kernel, far, last),
            [rows_out] * (len(far) + 1), [SM] + [VM] * (2 + len(far)),
            alias=[(3 + i, i) for i in range(len(far))],
        )(me1, places_other, whole, *[picked[k] for k in far])
        for at, k in enumerate(far):
            way = [(i, i ^ last ^ k if i in middle else i ^ k) for i in range(groups)]
            got[k] = lax.ppermute(onward[at], "grp", way)

        sketches = jnp.stack([sketches, swap_mem(sketches, 1)]).reshape(2, groups, *bin_sketch.shape)
        parts = [sketches]
        for q in range(1, chips):
            parts.append(swap_mem(sketches, 2 * q))
        each = bin_sketch.shape[0]
        (coarse,) = call(
            functools.partial(coarse_kernel, bin_sketch.shape[1] ** (-0.5)),
            [((groups * mems, each, rep_sketch.shape[0]), bf)],
            [SM] * 2 + [VM] * (1 + chips), mib=40 if groups * mems > 256 else 4,
            flops=2 * groups * mems * each * rep_sketch.size,
        )(me1, mine1, rep_sketch, *parts)
        coarse_scores = coarse.reshape(-1, rep_sketch.shape[0])

        shape = ((groups, chips, MOST, 128), f32)
        held = ()
        got[last] = through
        for keys in ([0], near + [last]):
            rows = [got[k] for k in keys] + ([direct] if last in keys else [])
            held = call(
                functools.partial(score_kernel, keys, last), [shape] * 2,
                [SM] * 2 + [VM] * (1 + len(rows) + len(held)),
                scratch=[pltpu.VMEM((slot_count, MOST * len(keys), members), f32)],
                mib=2,
                flops=2 * members * width_here * count * 8,
                alias=[(3 + len(rows) + i, i) for i in range(len(held))],
            )(me1, core1, member_profile, *rows, *held)
        keep, send = held

        def one_side(key, other, out):
            (out,) = call(
                functools.partial(half_kernel, key, other), [shape], [SM] * 2 + [VM] * 3,
                scratch=[pltpu.VMEM((MOST, members // 2), f32)], mib=2,
                flops=members * width_here * count * 8, alias=[(4, 0)],
            )(me1, core1, member_profile, got[key], out)
            return out

        for k in far:
            send = one_side(k, 1, send)
        send = swap_mem(send, 1)
        for k in far:
            keep = one_side(k, 0, keep)
        parts = keep + send
        parts = parts.reshape(groups * chips, MOST, 128)
        parts = lax.all_to_all(parts, ("grp", "chip"), 0, 0, tiled=True)
        parts = parts.reshape(groups, chips, MOST, 128)

        (fine,) = call(
            functools.partial(final_kernel, slot_count, FW ** (-0.5)),
            [((2, block, rows_here), f32)], [SM] + [VM] * 4,
        )(mine1, lines, slots_in, lives, parts)
        return (coarse_scores, fine.transpose(2, 0, 1))

    return local


def solution(mesh):
    groups, chips = mesh.shape["grp"], mesh.shape["mem"] // 2
    mesh = jax.sharding.Mesh(mesh.devices.reshape(groups, chips, 2), ("grp", "chip", "core"))
    mem = ("chip", "core")
    local = make_local(groups, chips)

    return jax.shard_map(
        local,
        mesh=mesh,
        in_specs=(
            P(("grp", *mem), None),
            P(("grp", *mem), None),
            P("grp", mem),
            P("grp", None, mem),
            P("grp", None),
            P(),
            P(),
        ),
        out_specs=(P(None, ("grp", *mem)), P("grp", None, mem)),
        check_vma=False,
    )
```

```python
import functools

import jax
import jax.numpy as jnp
from jax import lax
from jax.experimental import pallas as pl
from jax.experimental.pallas import tpu as pltpu
from jax.sharding import PartitionSpec as P


FW = 32768
MOST = 16
VM = pl.BlockSpec(memory_space=pltpu.VMEM)
SM = pl.BlockSpec(memory_space=pltpu.SMEM)
FAR = pl.BlockSpec(memory_space=pltpu.HBM)
NT = (((1,), (1,)), ((), ()))
NN = (((1,), (0,)), ((), ()))


def iota(shape, axis):
    return lax.broadcasted_iota(jnp.int32, shape, axis)


def hits(where, group, count):
    wanted = iota((count, where.shape[1]), 0) + group * count
    return (where[0:1] == wanted) | (where[1:2] == wanted)


def pick(hit, rows):
    one = hit.astype(jnp.float32).astype(jnp.bfloat16)
    return lax.dot_general(one, rows, NN, preferred_element_type=jnp.float32).astype(jnp.bfloat16)


def head_kernel(
    keys, slot_count, me, slots_far, sizes_far, routes_far, rows_far,
    places, lives, lines, slots_in, *refs,
):
    outs, (slots, sizes, routes, rows, sems) = refs[: len(keys)], refs[len(keys) :]
    pairs = ((slots_far, slots), (sizes_far, sizes), (routes_far, routes), (rows_far, rows))
    copies = [pltpu.make_async_copy(a, b, sems.at[i]) for i, (a, b) in enumerate(pairs)]
    for copy in copies:
        copy.start()
    total, count = slots.shape[0], outs[0].shape[0]
    width = routes.shape[1]
    before = (iota((width, width), 0) < iota((width, width), 1)).astype(jnp.float32)
    before = before.astype(jnp.bfloat16)
    cluster = iota((total, width), 0)
    slot_of = jnp.zeros((total, width), jnp.int32)
    size_of = jnp.zeros((total, width), jnp.int32)
    group_of = jnp.zeros((total, width), jnp.int32)
    for copy in copies[:3]:
        copy.wait()
    for c in range(total):
        slot_of = jnp.where(cluster == c, slots[c], slot_of)
        size_of = jnp.where(cluster == c, sizes[c], size_of)
        group_of = jnp.where(cluster == c, slots[c] // slot_count, group_of)
    seen = jnp.zeros((total, 1), jnp.float32)
    for r in range(2):
        hit = routes[r : r + 1] == cluster
        one = hit.astype(jnp.float32)
        earlier = lax.dot_general(
            one.astype(jnp.bfloat16), before, NN, preferred_element_type=jnp.float32
        )
        rank = jnp.sum(jnp.where(hit, earlier + seen, 0.0), axis=0, keepdims=True)
        seen = seen + jnp.sum(one, axis=1, keepdims=True)
        slot = jnp.sum(jnp.where(hit, slot_of, 0), axis=0, keepdims=True)
        group = jnp.sum(jnp.where(hit, group_of, 0), axis=0, keepdims=True)
        places[r : r + 1] = slot * MOST + rank.astype(jnp.int32)
        lines[r : r + 1] = group * MOST + rank.astype(jnp.int32)
        slots_in[r : r + 1] = slot - group * slot_count
        lives[r : r + 1] = jnp.sum(jnp.where(hit, size_of, 0), axis=0, keepdims=True)
    where = places[...]
    copies[3].wait()
    for key, out in zip(keys, outs, strict=True):
        out[...] = pick(hits(where, me[0] ^ key, count), rows[...])


def is_inner(me, last):
    return (me[0] == last // 2) | (me[0] == last // 2 + 1)


def forward_kernel(keys, last, me, places_other, whole, *refs):
    outs = refs[len(keys) :]
    count = outs[0].shape[0]

    @pl.when(is_inner(me, last))
    def _():
        where = places_other[...]
        for key, out in zip(keys, outs):
            out[...] = pick(hits(where, me[0] ^ last ^ key, count), whole[...])
        outs[-1][...] = pick(hits(where, me[0], count), whole[...])


def score_kernel(keys, last, me, core, members, *refs):
    keep, send, acc = refs[-3:]
    ins = list(refs[: len(keys) + (last in keys)])
    slot_count, total, _ = members.shape
    chips = keep.shape[1]
    block = total // (2 * chips)

    def put(ins):
        for s in range(slot_count):
            rows = [src[s * MOST : (s + 1) * MOST, :] for src in ins]
            rows = jnp.concatenate(rows, axis=0) if len(rows) > 1 else rows[0]
            product = lax.dot_general(members[s], rows, NT, preferred_element_type=jnp.float32)
            acc[s] = product.T

    def give(first, second):
        for at, key in enumerate(keys):
            for chip in range(chips):
                for side, out in enumerate((first, second)):
                    start = (chip * 2 + side) * block
                    for s in range(slot_count):
                        out[me[0] ^ key, chip, :, s * block : (s + 1) * block] = (
                            acc[s, at * MOST : (at + 1) * MOST, start : start + block]
                        )

    if last in keys:
        inner = is_inner(me, last)
        pl.when(inner)(lambda: put(ins[:-1]))
        pl.when(jnp.logical_not(inner))(lambda: put(ins[:-2] + ins[-1:]))
    else:
        put(ins)
    pl.when(core[0] == 0)(lambda: give(keep, send))
    pl.when(core[0] == 1)(lambda: give(send, keep))


def coarse_kernel(scale, me, mine, reps, *refs):
    parts, out = refs[:-1], refs[-1]
    cores, groups, each, width = parts[0].shape
    mems = cores * len(parts)
    lines = cores * groups
    batch = max(1, 256 // (lines * each))
    for first in range(0, len(parts), batch):
        rows = [part[...].reshape(lines * each, width) for part in parts[first : first + batch]]
        rows = jnp.concatenate(rows, axis=0) if len(rows) > 1 else rows[0]
        score = lax.dot_general(rows, reps[...], NT, preferred_element_type=jnp.float32)
        score = (score * scale).astype(out.dtype)
        for at in range(score.shape[0] // each):
            member = mine[0] ^ (first * cores + at // groups)
            out[(me[0] ^ (at % groups)) * mems + member] = score[at * each : (at + 1) * each]


def half_kernel(key, other, me, core, members, rows, _, out):
    slot_count, chips = members.shape[0], out.shape[1]
    block = members.shape[1] // (2 * chips)
    starts = [pl.multiple_of((chip * 2 + (core[0] ^ other)) * block, block) for chip in range(chips)]
    for s in range(slot_count):
        half = jnp.concatenate([members[s, pl.ds(start, block), :] for start in starts], axis=0)
        product = lax.dot_general(
            rows[s * MOST : (s + 1) * MOST, :], half, NT, preferred_element_type=jnp.float32
        )
        for chip in range(chips):
            out[me[0] ^ key, chip, :, s * block : (s + 1) * block] = (
                product[:, chip * block : (chip + 1) * block]
            )


def final_kernel(slot_count, scale, mine, lines, slots, lives, parts, out):
    groups, chips = parts.shape[:2]
    block, rows = out.shape[1], out.shape[2]
    member = iota((block, rows), 0) + mine[0] * block
    total = parts[:, 0]
    for chip in range(1, chips):
        total = total + parts[:, chip]
    total = total.reshape(groups * MOST, total.shape[2])
    line = jnp.concatenate([lines[r : r + 1] for r in range(2)], axis=1)
    one = (line == iota((groups * MOST, 2 * rows), 0)).astype(jnp.float32).astype(jnp.bfloat16)
    score = jnp.zeros((total.shape[1], 2 * rows), jnp.float32)
    for _ in range(3):
        piece = total.astype(jnp.bfloat16)
        total = total - piece.astype(jnp.float32)
        score = score + lax.dot_general(
            piece, one, (((0,), (0,)), ((), ())), preferred_element_type=jnp.float32
        )
    for r in range(2):
        slot = slots[r : r + 1]
        found = jnp.zeros((block, rows), jnp.float32)
        for s in range(slot_count):
            part = score[s * block : (s + 1) * block, r * rows : (r + 1) * rows]
            found = jnp.where(slot == s, part, found)
        out[r] = jnp.where(member < lives[r : r + 1], found * scale, 0.0)


def call(kernel, shapes, specs, scratch=(), flops=0, mib=4, alias=()):
    return pl.pallas_call(
        kernel,
        out_shape=[jax.ShapeDtypeStruct(s, d) for s, d in shapes],
        in_specs=specs,
        out_specs=[VM] * len(shapes),
        scratch_shapes=scratch,
        input_output_aliases=dict(alias),
        compiler_params=pltpu.CompilerParams(vmem_limit_bytes=mib << 20),
        cost_estimate=pl.CostEstimate(flops=flops, bytes_accessed=1 << 18, transcendentals=0),
    )


def stay(value):
    return pltpu.with_memory_space_constraint(value, pltpu.HBM)


def make_local(groups, chips):
    last = groups - 1
    half = groups // 2
    middle = (half - 1, half)
    mems = 2 * chips

    def swap(value, key):
        return lax.ppermute(value, "grp", [(i, i ^ key) for i in range(groups)])

    def swap_mem(value, key):
        if key == 1:
            return lax.ppermute(value, "core", [(0, 1), (1, 0)])
        return lax.ppermute(value, "chip", [(i, i ^ (key // 2)) for i in range(chips)])

    def local(
        bin_sketch, rep_sketch, bin_profile, member_profile, bin_routes, owner_slot, cluster_sizes
    ):
        rows_here, width_here = bin_profile.shape
        slot_count, members, _ = member_profile.shape
        count = slot_count * MOST
        block = members // mems
        me = lax.axis_index("grp")
        core = lax.axis_index("core")
        mine = lax.axis_index("chip") * 2 + core
        member_profile = pltpu.with_memory_space_constraint(member_profile, pltpu.VMEM)
        me1, mine1, core1 = me.reshape(1), mine.reshape(1), core.reshape(1)
        bf, f32, i32 = jnp.bfloat16, jnp.float32, jnp.int32
        rows_out = ((count, width_here), bf)

        whole = lax.ppermute(bin_profile, "grp", [(i, i ^ last) for i in middle])

        near = list(range(1, half))
        far = list(range(half, last))
        keys = near + [last] + far + [0]
        total = owner_slot.shape[0]
        places, lives, lines, slots_in, *picked = call(
            functools.partial(head_kernel, keys, slot_count),
            [((2, rows_here), i32)] * 4 + [rows_out] * len(keys),
            [SM] + [FAR] * 4,
            scratch=[
                pltpu.SMEM((total,), i32), pltpu.SMEM((total,), i32),
                pltpu.VMEM((2, rows_here), i32), pltpu.VMEM(bin_profile.shape, bf),
                pltpu.SemaphoreType.DMA((4,)),
            ],
        )(me1, *[stay(x) for x in (owner_slot, cluster_sizes, bin_routes.T, bin_profile)])
        picked = dict(zip(keys, picked, strict=True))
        places_other = lax.ppermute(places, "grp", [(i, i ^ last) for i in middle])

        sketches = bin_sketch[None]
        step = 1
        while step < groups:
            sketches = jnp.concatenate([sketches, swap(sketches, step)])
            step *= 2

        got = {0: picked[0]}
        for k in near:
            got[k] = swap(picked[k], k)
        outer = [(i, i ^ last) for i in range(groups) if i not in middle]
        direct = lax.ppermute(picked[last], "grp", outer)
        *onward, through = call(
            functools.partial(forward_kernel, far, last),
            [rows_out] * (len(far) + 1), [SM] + [VM] * (2 + len(far)),
            alias=[(3 + i, i) for i in range(len(far))],
        )(me1, places_other, whole, *[picked[k] for k in far])
        for at, k in enumerate(far):
            way = [(i, i ^ last ^ k if i in middle else i ^ k) for i in range(groups)]
            got[k] = lax.ppermute(onward[at], "grp", way)

        sketches = jnp.stack([sketches, swap_mem(sketches, 1)]).reshape(2, groups, *bin_sketch.shape)
        parts = [sketches]
        for q in range(1, chips):
            parts.append(swap_mem(sketches, 2 * q))
        each = bin_sketch.shape[0]
        (coarse,) = call(
            functools.partial(coarse_kernel, bin_sketch.shape[1] ** (-0.5)),
            [((groups * mems, each, rep_sketch.shape[0]), bf)],
            [SM] * 2 + [VM] * (1 + chips), mib=40 if groups * mems > 256 else 4,
            flops=2 * groups * mems * each * rep_sketch.size,
        )(me1, mine1, rep_sketch, *parts)
        coarse_scores = coarse.reshape(-1, rep_sketch.shape[0])

        shape = ((groups, chips, MOST, 128), f32)
        held = ()
        got[last] = through
        for keys in ([0], near + [last]):
            rows = [got[k] for k in keys] + ([direct] if last in keys else [])
            held = call(
                functools.partial(score_kernel, keys, last), [shape] * 2,
                [SM] * 2 + [VM] * (1 + len(rows) + len(held)),
                scratch=[pltpu.VMEM((slot_count, MOST * len(keys), members), f32)],
                mib=2,
                flops=2 * members * width_here * count * 8,
                alias=[(3 + len(rows) + i, i) for i in range(len(held))],
            )(me1, core1, member_profile, *rows, *held)
        keep, send = held

        def one_side(key, other, out):
            (out,) = call(
                functools.partial(half_kernel, key, other), [shape], [SM] * 2 + [VM] * 3,
                mib=2,
                flops=members * width_here * count * 8, alias=[(4, 0)],
            )(me1, core1, member_profile, got[key], out)
            return out

        for k in far:
            send = one_side(k, 1, send)
        send = swap_mem(send, 1)
        for k in far:
            keep = one_side(k, 0, keep)
        parts = keep + send
        parts = parts.reshape(groups * chips, MOST, 128)
        parts = lax.all_to_all(parts, ("grp", "chip"), 0, 0, tiled=True)
        parts = parts.reshape(groups, chips, MOST, 128)

        (fine,) = call(
            functools.partial(final_kernel, slot_count, FW ** (-0.5)),
            [((2, block, rows_here), f32)], [SM] + [VM] * 4,
        )(mine1, lines, slots_in, lives, parts)
        return (coarse_scores, fine.transpose(2, 0, 1))

    return local


def solution(mesh):
    groups, chips = mesh.shape["grp"], mesh.shape["mem"] // 2
    mesh = jax.sharding.Mesh(mesh.devices.reshape(groups, chips, 2), ("grp", "chip", "core"))
    mem = ("chip", "core")
    local = make_local(groups, chips)

    return jax.shard_map(
        local,
        mesh=mesh,
        in_specs=(
            P(("grp", *mem), None),
            P(("grp", *mem), None),
            P("grp", mem),
            P("grp", None, mem),
            P("grp", None),
            P(),
            P(),
        ),
        out_specs=(P(None, ("grp", *mem)), P("grp", None, mem)),
        check_vma=False,
    )
```
